32 devices in a mesh: section: 8 (over y, x, core), tensor: 4 (over z).
Axes of the slice: x: 2, y: 2, z: 4, core: 2. Of those that a mesh axis runs over, the one named last changes fastest.
Arguments:
- frozen: bfloat16 [8, 14336, 2048], P('section', 'tensor'), may hold values from -1 to 1, as said below
- adapter_a: bfloat16 [8, 8, 14336], P('section', None, 'tensor'), may hold values from -0.119628906 to 0.119628906
- adapter_b: bfloat16 [8, 16, 2048], P('section'), may hold values from -0.22460938 to 0.22460938
- magnitude: float32 [8, 2048], P('section'), may hold values from 0.5 to 2
- hidden_fwd: bfloat16 [8, 128, 14336], P('section', None, 'tensor'), may hold values from -6 to 6
- carried: bfloat16 [8, 256, 2048], P('section', 'tensor'), may hold values from -6 to 6
- embedded: bfloat16 [256, 4096], P('tensor'), may hold values from -6 to 6
- hidden_bwd: bfloat16 [8, 128, 14336], P('section', None, 'tensor'), may hold values from -6 to 6
- returned: bfloat16 [8, 256, 2048], P('section', 'tensor'), may hold values from -1.5 to 1.5
- head_grad: bfloat16 [256, 4096], P('tensor'), may hold values from -1.5 to 1.5
Outputs:
- section_out: bfloat16 [8, 256, 2048], P('section', 'tensor')
- grad_magnitude: float32 [8, 2048], P('section')
- grad_a: float32 [8, 8, 14336], P('section', None, 'tensor')
- grad_b: float32 [8, 16, 2048], P('section')
- hidden_grad: bfloat16 [8, 128, 14336], P('section', None, 'tensor')
The draws below stay inside these ranges and needn't reach their ends.
Inputs may be any that keep to these rules, and one draw needn't show every extreme that they name: frozen projection weights.
All inputs are finite; a program needn't handle non-finite values.
Results may differ from the reference program's by a relative error of at most 0.0057.
Values may be sent and summed in bfloat16 or wider, within the bound.
No kernel may reach another device: no remote copies, remote signals or barrier semaphores. Data moves between devices by JAX's collectives and lax.ppermute only.
A program may use at most 128 MiB of HBM per device.

```python
import math
import jax
import jax.numpy as jnp
from jax import lax

D = 4096
FF = 14336
R = 16
T_SIZE = 256
SECTIONS = 4
SLOTS = 8


def draw_frozen(key, part):

    def one_slot(slot_num):
        slot_key = jax.random.fold_in(jax.random.fold_in(key, 7001), slot_num)
        key_base, key_rows, key_cols = jax.random.split(slot_key, 3)
        base = jax.random.normal(key_base, (FF, D // 2), jnp.float32)
        slope = 0.55
        row_gain = jnp.exp(jax.random.uniform(key_rows, (FF, 1), jnp.float32, minval=-1.15, maxval=1.15))
        col_gain = jnp.exp(jax.random.uniform(key_cols, (1, D // 2), jnp.float32, minval=-1.15, maxval=1.15))
        trend = jnp.exp(slope * jnp.arange(FF, dtype=jnp.float32) / FF)[:, None]
        row_total = row_gain * trend
        normal_by = jnp.sqrt(jnp.sum(row_total * row_total))
        values = jnp.clip(base * row_total * col_gain / normal_by, -1.0, 1.0)
        return values.astype(jnp.bfloat16)
    return lax.map(one_slot, jnp.arange(SLOTS))


def block_scale(own_key, dims, cuts, low, largest):
    level = 1.0
    for position, shards_of in cuts:
        draws = jax.random.uniform(jax.random.fold_in(jax.random.fold_in(own_key, 6), position), (shards_of,), jnp.float32, low / len(cuts), largest / len(cuts))
        level = level * jnp.repeat(jnp.exp(draws), dims[position] // shards_of).reshape((-1,) + (1,) * (len(dims) - 1 - position))
    return level


def centred(rng, shape, spread, most, shards=(), held_as=jnp.bfloat16):
    result = jax.random.normal(rng, shape, jnp.float32) * spread
    if len(shards) > 0:
        result = block_scale(rng, shape, shards, -0.22, 0.18) * result
    return jnp.clip(result, min=-most, max=most).astype(held_as)


def setup_inputs(seed: int = 0) -> dict:
    key_list = jax.random.split(jax.random.key(seed), 11)
    return {
        "frozen": draw_frozen(jax.random.fold_in(key_list[10], 71), 0),
        "adapter_a": centred(key_list[1], (SLOTS, R // 2, FF), 0.02, 0.119628906, ((0, 8), (2, 4))),
        "adapter_b": centred(key_list[2], (SLOTS, R, D // 2), 0.0375, 0.22460938, ((0, 8),)),
        "magnitude": jnp.clip(jnp.exp(math.log(2.0) - 1.3862944 * jax.random.uniform(key_list[3], (SLOTS, D // 2), jnp.float32) ** block_scale(key_list[3], (SLOTS, D // 2), ((0, 8),), -0.2, 0.2)), 0.5, 2.0),
        "hidden_fwd": centred(key_list[4], (SLOTS, T_SIZE // 2, FF), 1.0, 6.0, ((0, 8), (2, 4))),
        "carried": centred(key_list[5], (SLOTS, T_SIZE, D // 2), 1.0, 6.0, ((0, 8), (1, 4))),
        "embedded": centred(key_list[6], (T_SIZE, D), 1.0, 6.0, ((0, 4),)),
        "hidden_bwd": centred(key_list[7], (SLOTS, T_SIZE // 2, FF), 1.0, 6.0, ((0, 8), (2, 4))),
        "returned": centred(key_list[8], (SLOTS, T_SIZE, D // 2), 0.25, 1.5, ((0, 8), (1, 4))),
        "head_grad": centred(key_list[9], (T_SIZE, D), 0.25, 1.5, ((0, 4),)),
    }


epsilon = 1e-06

def one_section(packed):
    base_pair, fac_a, fac_pair, mag, hid_fwd, inflow, hid_bwd, cot = packed
    base_w = jnp.concatenate([base_pair[0], base_pair[1]], axis=1)
    fac_b = jnp.concatenate([fac_pair[0], fac_pair[1]], axis=1)
    merged = (base_w.astype(jnp.float32) + jnp.dot(fac_a.T, fac_b, preferred_element_type=jnp.float32)).astype(jnp.bfloat16)
    merged_f = merged.astype(jnp.float32)
    col_norms = jnp.sqrt(lax.optimization_barrier(jnp.sum(merged_f * merged_f, axis=0)) + epsilon)
    col_scale = mag / col_norms
    projected = jnp.dot(hid_fwd, merged, preferred_element_type=jnp.float32)
    section_out = (inflow.astype(jnp.float32) + projected * col_scale).astype(jnp.bfloat16)
    low = jnp.dot(hid_bwd, fac_a.T, preferred_element_type=jnp.float32).astype(jnp.bfloat16)
    recomputed = jnp.dot(hid_bwd, merged, preferred_element_type=jnp.float32)
    grad_mag = lax.optimization_barrier(jnp.sum(cot.astype(jnp.float32) * recomputed, axis=0)) / col_norms
    scaled_cot = (cot.astype(jnp.float32) * col_scale).astype(jnp.bfloat16)
    hidden_grad = jnp.dot(scaled_cot, merged.T, preferred_element_type=jnp.float32).astype(jnp.bfloat16)
    adapter_cot = jnp.dot(scaled_cot, fac_b.T, preferred_element_type=jnp.float32).astype(jnp.bfloat16)
    grad_a = jnp.dot(adapter_cot.T, hid_bwd, preferred_element_type=jnp.float32)
    grad_b = jnp.dot(low.T, scaled_cot, preferred_element_type=jnp.float32)
    return (section_out, grad_mag, grad_a, grad_b, hidden_grad)

def join_cols(values):
    paired = values.reshape((SECTIONS, 2) + values.shape[1:])
    return jnp.concatenate([paired[:, 0], paired[:, 1]], axis=-1)

def split_cols(values):
    half = values.shape[-1] // 2
    stacked = jnp.stack([values[..., :half], values[..., half:]], axis=1)
    return stacked.reshape((SECTIONS * 2,) + values.shape[1:-1] + (half,))

def reference(frozen, adapter_a, adapter_b, magnitude, hidden_fwd, carried, embedded, hidden_bwd, returned, head_grad):
    base_pairs = frozen.reshape((SECTIONS, 2) + frozen.shape[1:])
    fac_pairs = adapter_b.reshape((SECTIONS, 2) + adapter_b.shape[1:])
    fac_a = adapter_a.reshape((SECTIONS, R, FF))
    mag = magnitude.reshape((SECTIONS, D))
    hid_fwd = hidden_fwd.reshape((SECTIONS, T_SIZE, FF))
    hid_bwd = hidden_bwd.reshape((SECTIONS, T_SIZE, FF))
    carried_full = join_cols(carried)
    returned_full = join_cols(returned)
    inflow = jnp.concatenate([embedded[None], carried_full[:-1]], axis=0)
    cot = jnp.concatenate([returned_full[1:], head_grad[None]], axis=0)
    section_out, grad_mag, grad_a, grad_b, hidden_grad = lax.map(one_section, (base_pairs, fac_a, fac_pairs, mag, hid_fwd, inflow, hid_bwd, cot))
    return (split_cols(section_out), grad_mag.reshape((SECTIONS * 2, D // 2)), grad_a.reshape((SECTIONS * 2, R // 2, FF)), split_cols(grad_b), hidden_grad.reshape((SECTIONS * 2, T_SIZE // 2, FF)))
```

```python
import functools

import jax
import jax.numpy as jnp
from jax import lax
from jax.experimental import pallas as pl
from jax.experimental.pallas import tpu as pltpu
from jax.sharding import PartitionSpec as P

epsilon = 1e-06
f32 = jnp.float32
bf16 = jnp.bfloat16
NT = (((1,), (1,)), ((), ()))
TN = (((0,), (0,)), ((), ()))


def block_of(size, most):
    return max(b for b in range(128, most + 1, 128) if size % b == 0)


def dot(a, b, dims=(((1,), (0,)), ((), ()))):
    return lax.dot_general(a, b, dims, preferred_element_type=f32)


def two_parts(value):
    high = value.astype(bf16)
    low = (value - high.astype(f32)).astype(bf16)
    return jnp.concatenate([high, low], axis=1)


def halves(own, other, half):
    own, other = own.astype(f32), other.astype(f32)
    first = jnp.where(half == 0, own, other)
    second = jnp.where(half == 0, other, own)
    return jnp.concatenate([first, second], axis=0).astype(bf16)


def place_of(shard, half, count):
    return jnp.bitwise_xor(shard, half * (count // 2))


def forward_kernel(
    count, rows, xo, xt, yo, yt, ao, at, b, w, *refs
):
    outs, pack = refs[:count], refs[count]
    xs, lx, gram, res = refs[count + 1 :]
    half = lax.axis_index("section") % 2
    me = lax.axis_index("tensor")
    step = pl.program_id(0)
    tokens = 2 * xo.shape[0]
    rank = b.shape[0]
    lines = pack.shape[0] - rank

    @pl.when(step == 0)
    def _():
        fac = halves(ao[...], at[...], half)
        xs[: tokens // 2, :] = xo[...]
        xs[tokens // 2 : tokens, :] = xt[...]
        xs[tokens:, :] = fac
        lx[...] = two_parts(dot(xs[:tokens, :], fac, NT))
        gram[...] = two_parts(dot(fac, fac, NT))
        low = jnp.concatenate([dot(yo[...], fac, NT), dot(yt[...], fac, NT)], axis=0)
        pack[lines:, :] = low.T

    wv = w[...]
    both_b = jnp.concatenate([b[...], b[...]], axis=0)
    total = dot(xs[...], wv)
    res[...] = total[:tokens] + dot(lx[...], both_b)
    wf = wv.astype(f32)
    squares = jnp.sum((wf * wf).reshape(wf.shape[0] // 8, 8, wf.shape[1]), axis=0)
    cross = 2.0 * total[tokens:] + dot(gram[...], both_b)
    cross = b[...].astype(f32) * cross
    for r in range(0, rank, 8):
        squares = squares + cross[r : r + 8]
    squares = jnp.sum(squares, axis=0, keepdims=True)
    across = pack.shape[1]
    many = wv.shape[1] // across
    for i in range(many):
        pack[pl.ds(step * many + i, 1), :] = squares[:, i * across : (i + 1) * across]
    for k in range(count):
        at_row = place_of(jnp.bitwise_xor(me, k), half, count) * rows
        piece = res[pl.ds(pl.multiple_of(at_row, rows), rows), :]
        outs[k][...] = piece.astype(outs[k].dtype)


def forward(count, rows, xo, xt, yo, yt, ao, at, b, w):
    ff, width = w.shape
    tokens = 2 * xo.shape[0]
    rank = b.shape[0]
    nb = block_of(width, 512)
    whole = lambda a: pl.BlockSpec(a.shape, lambda j: (0, 0))
    lines = width // tokens
    shapes = [jax.ShapeDtypeStruct((rows, width), f32 if k == 0 else bf16) for k in range(count)]
    return pl.pallas_call(
        functools.partial(forward_kernel, count, rows),
        grid=(width // nb,),
        in_specs=[whole(a) for a in (xo, xt, yo, yt, ao, at)]
        + [pl.BlockSpec((rank, nb), lambda j: (0, j)), pl.BlockSpec((ff, nb), lambda j: (0, j))],
        out_specs=[pl.BlockSpec((rows, nb), lambda j: (0, j)) for _ in range(count)]
        + [pl.BlockSpec((lines + rank, tokens), lambda j: (0, 0))],
        out_shape=shapes + [jax.ShapeDtypeStruct((lines + rank, tokens), f32)],
        scratch_shapes=[
            pltpu.VMEM((tokens + rank, ff), bf16),
            pltpu.VMEM((tokens, 2 * rank), bf16),
            pltpu.VMEM((rank, 2 * rank), bf16),
            pltpu.VMEM((tokens, nb), f32),
        ],
        name="forward",
        cost_estimate=pl.CostEstimate(
            flops=2 * tokens * ff * width, bytes_accessed=2 * ff * width, transcendentals=0
        ),
    )(xo, xt, yo, yt, ao, at, b, w)


def again_kernel(yo, yt, pack, b, w, out, ys, ly):
    half_tokens = yo.shape[0]
    rank = b.shape[0]

    @pl.when(pl.program_id(0) == 0)
    def _():
        ys[:half_tokens, :] = yo[...]
        ys[half_tokens:, :] = yt[...]
        ly[...] = two_parts(pack[pack.shape[0] - rank :, :].T)

    both_b = jnp.concatenate([b[...], b[...]], axis=0)
    out[...] = dot(ys[...], w[...]) + dot(ly[...], both_b)


def again(yo, yt, pack, b, w):
    ff, width = w.shape
    tokens = 2 * yo.shape[0]
    rank = b.shape[0]
    nb = block_of(width, 512)
    whole = lambda a: pl.BlockSpec(a.shape, lambda j: (0, 0))
    return pl.pallas_call(
        again_kernel,
        grid=(width // nb,),
        in_specs=[whole(a) for a in (yo, yt, pack)]
        + [pl.BlockSpec((rank, nb), lambda j: (0, j)), pl.BlockSpec((ff, nb), lambda j: (0, j))],
        out_specs=pl.BlockSpec((tokens, nb), lambda j: (0, j)),
        out_shape=jax.ShapeDtypeStruct((tokens, width), f32),
        scratch_shapes=[pltpu.VMEM((tokens, ff), bf16), pltpu.VMEM((tokens, 2 * rank), bf16)],
        name="again",
        cost_estimate=pl.CostEstimate(
            flops=2 * tokens * ff * width, bytes_accessed=2 * ff * width, transcendentals=0
        ),
    )(yo, yt, pack, b, w)


def backward_kernel(count, rows, *refs):
    cots, packs = refs[:count], refs[count : 2 * count]
    mag, r, b, ao, at, w = refs[2 * count : 2 * count + 6]
    own, send, adapt, gb, magpack, norms = refs[2 * count + 6 : 2 * count + 12]
    sc, ad = refs[2 * count + 12 :]
    half = lax.axis_index("section") % 2
    me = lax.axis_index("tensor")
    rank = b.shape[0]
    tokens, width = sc.shape

    @pl.when(pl.program_id(0) == 0)
    def _():
        total = packs[0][...]
        for k in range(1, count):
            total = total + packs[k][...]
        lines = total.shape[0] - rank
        across = total.shape[1]
        sqr = jnp.sqrt(jnp.maximum(total[:lines], 0.0) + epsilon)
        for i in range(lines):
            norms[0:1, i * across : (i + 1) * across] = sqr[i : i + 1, :]
        scale = mag[...] / norms[0:1, :]
        norms[1:2, :] = scale
        mags = jnp.zeros((8, width), f32)
        for k in range(count):
            at_row = place_of(jnp.bitwise_xor(me, k), half, count) * rows
            spot = pl.ds(pl.multiple_of(at_row, rows), rows)
            cot = cots[k][...].astype(f32)
            sc[spot, :] = (cot * scale).astype(bf16)
            mags = mags + jnp.sum((cot * r[spot, :]).reshape(rows // 8, 8, width), axis=0)
        mags = jnp.sum(mags, axis=0, keepdims=True)
        for i in range(lines):
            magpack[i : i + 1, :] = mags[:, i * across : (i + 1) * across]
        part = dot(sc[...], b[...], NT)
        adapt[...] = part
        ad[...] = two_parts(part)
        low = total[lines:].astype(bf16)
        gb[...] = dot(low, sc[...])

    fac = halves(ao[...], at[...], half)
    both_a = jnp.concatenate([fac, fac], axis=0)
    out = dot(sc[...], w[...], NT) + dot(ad[...], both_a)
    own[...] = out[: tokens // 2]
    send[...] = out[tokens // 2 :].astype(bf16)


def backward(count, rows, cots, packs, mag, r, b, ao, at, w):
    ff, width = w.shape
    tokens = rows * count
    rank = b.shape[0]
    rb = block_of(ff, 512)
    lines = packs[0].shape[0] - rank
    whole = lambda a: pl.BlockSpec(a.shape, lambda j: (0, 0))
    fixed = lambda shape: pl.BlockSpec(shape, lambda j: (0, 0))
    cols = lambda m: pl.BlockSpec((m, rb), lambda j: (0, j))
    return pl.pallas_call(
        functools.partial(backward_kernel, count, rows),
        grid=(ff // rb,),
        in_specs=[whole(a) for a in (*cots, *packs, mag, r, b)]
        + [cols(rank // 2), cols(rank // 2), pl.BlockSpec((rb, width), lambda j: (j, 0))],
        out_specs=[
            cols(tokens // 2),
            cols(tokens // 2),
            fixed((tokens, rank)),
            fixed((rank, width)),
            fixed((lines, tokens)),
            fixed((2, width)),
        ],
        out_shape=[
            jax.ShapeDtypeStruct((tokens // 2, ff), f32),
            jax.ShapeDtypeStruct((tokens // 2, ff), bf16),
            jax.ShapeDtypeStruct((tokens, rank), f32),
            jax.ShapeDtypeStruct((rank, width), f32),
            jax.ShapeDtypeStruct((lines, tokens), f32),
            jax.ShapeDtypeStruct((2, width), f32),
        ],
        scratch_shapes=[pltpu.VMEM((tokens, width), bf16), pltpu.VMEM((tokens, 2 * rank), bf16)],
        name="backward",
        cost_estimate=pl.CostEstimate(
            flops=2 * tokens * ff * width, bytes_accessed=2 * ff * width, transcendentals=0
        ),
    )(*cots, *packs, mag, r, b, ao, at, w)


def emit_kernel(count, *refs):
    parts = refs[:count]
    carried, embedded, norms, out = refs[count:]
    slot = lax.axis_index("section")
    half = slot % 2
    width = out.shape[1]
    here = embedded[:, pl.ds(pl.multiple_of(half * width, width), width)].astype(f32)
    inflow = jnp.where(slot < 2, here, carried[...].astype(f32))
    total = parts[0][...]
    for k in range(1, count):
        total = total + parts[k][...].astype(f32)
    out[...] = (inflow + total * norms[1:2, :]).astype(bf16)


def emit(count, parts, carried, embedded, norms):
    return pl.pallas_call(
        functools.partial(emit_kernel, count),
        out_shape=jax.ShapeDtypeStruct(carried.shape, bf16),
        name="emit",
    )(*parts, carried, embedded, norms)


def finish_kernel(count, *refs):
    own, got, adapt, got_adapt, yo, yt = refs[:6]
    mags = refs[6 : 6 + count]
    norms = refs[6 + count]
    hidden, ga, gm = refs[7 + count :]
    half = lax.axis_index("section") % 2
    hidden[...] = (own[...] + got[...].astype(f32)).astype(bf16)
    tokens, rank = adapt.shape
    ht, hr = tokens // 2, rank // 2
    first = adapt[:ht, :] + got_adapt[ht:, :]
    second = adapt[ht:, :] + got_adapt[:ht, :]
    pick = lambda v: jnp.where(half == 0, v[:, :hr], v[:, hr:]).astype(bf16)
    ga[...] = dot(pick(first), yo[...], TN) + dot(pick(second), yt[...], TN)

    @pl.when(pl.program_id(0) == 0)
    def _():
        total = mags[0][...]
        for k in range(1, count):
            total = total + mags[k][...]
        across = total.shape[1]
        for i in range(total.shape[0]):
            cut = slice(i * across, (i + 1) * across)
            gm[:, cut] = total[i : i + 1, :] / norms[0:1, cut]


def finish(count, own, got, adapt, got_adapt, yo, yt, mags, norms):
    ht, ff = own.shape
    rank = adapt.shape[1]
    rb = block_of(ff, 1792)
    whole = lambda a: pl.BlockSpec(a.shape, lambda j: (0, 0))
    cols = lambda m: pl.BlockSpec((m, rb), lambda j: (0, j))
    return pl.pallas_call(
        functools.partial(finish_kernel, count),
        grid=(ff // rb,),
        in_specs=[cols(ht), cols(ht), whole(adapt), whole(got_adapt), cols(ht), cols(ht)]
        + [whole(a) for a in (*mags, norms)],
        out_specs=[
            cols(ht),
            cols(rank // 2),
            pl.BlockSpec((1, norms.shape[1]), lambda j: (0, 0)),
        ],
        out_shape=[
            jax.ShapeDtypeStruct((ht, ff), bf16),
            jax.ShapeDtypeStruct((rank // 2, ff), f32),
            jax.ShapeDtypeStruct((1, norms.shape[1]), f32),
        ],
        name="finish",
    )(own, got, adapt, got_adapt, yo, yt, *mags, norms)


def local(
    frozen,
    adapter_a,
    adapter_b,
    magnitude,
    hidden_fwd,
    carried,
    embedded,
    hidden_bwd,
    returned,
    head_grad,
):
    w, ao, b, xo, yo = frozen[0], adapter_a[0], adapter_b[0], hidden_fwd[0], hidden_bwd[0]
    slots = lax.axis_size("section")
    count = lax.axis_size("tensor")
    slot = lax.axis_index("section")
    half = slot % 2
    rows, width = carried.shape[1:]

    def swap(array):
        return lax.ppermute(array, "section", [(i, i ^ 1) for i in range(slots)])

    def across(array, k):
        return lax.ppermute(array, "tensor", [(i, i ^ k) for i in range(count)])

    def shift(array, k):
        pairs = [
            (((s + 2) % slots) * count + t, s * count + (t ^ k))
            for s in range(slots)
            for t in range(count)
        ]
        return lax.ppermute(array, ("section", "tensor"), pairs)

    head = lax.dynamic_slice_in_dim(head_grad, half * width, width, 1)
    leaving = jnp.where(slot < 2, head, returned[0])
    xt, at, yt = swap(xo), swap(ao), swap(yo)
    cots = [None] * count
    for k in range(0, count, 2):
        cots[k] = shift(leaving, k)
        cots[k + 1] = across(cots[k], 1)
    arriving = lax.ppermute(carried[0], "section", [(i, i + 2) for i in range(slots - 2)])

    *parts, pack = forward(count, rows, xo, xt, yo, yt, ao, at, b, w)
    packs = [pack] + [across(pack, k) for k in range(1, count)]
    parts = [parts[0]] + [across(parts[k], k) for k in range(1, count)]
    r = again(yo, yt, pack, b, w)
    own, send, adapt, gb, magpack, norms = backward(
        count, rows, cots, packs, magnitude, r, b, ao, at, w
    )
    got, got_adapt = swap(send), swap(adapt)
    mags = [magpack] + [across(magpack, k) for k in range(1, count)]
    out = emit(count, parts, arriving, embedded, norms)
    hidden, ga, gm = finish(count, own, got, adapt, got_adapt, yo, yt, mags, norms)
    return (out[None], gm, ga[None], gb[None], hidden[None])


def solution(mesh):
    placed = (
        P("section", "tensor", None),
        P("section", None, "tensor"),
        P("section", None, None),
        P("section", None),
        P("section", None, "tensor"),
        P("section", "tensor", None),
        P("tensor", None),
        P("section", None, "tensor"),
        P("section", "tensor", None),
        P("tensor", None),
    )
    return jax.shard_map(
        local,
        mesh=mesh,
        in_specs=placed,
        out_specs=(
            P("section", "tensor", None),
            P("section", None),
            P("section", None, "tensor"),
            P("section", None, None),
            P("section", None, "tensor"),
        ),
        check_vma=False,
    )
```

```python
import functools

import jax
import jax.numpy as jnp
from jax import lax
from jax.experimental import pallas as pl
from jax.experimental.pallas import tpu as pltpu
from jax.sharding import PartitionSpec as P

epsilon = 1e-06
f32 = jnp.float32
bf16 = jnp.bfloat16
NT = (((1,), (1,)), ((), ()))
TN = (((0,), (0,)), ((), ()))


def block_of(size, most):
    return max(b for b in range(128, most + 1, 128) if size % b == 0)


def dot(a, b, dims=(((1,), (0,)), ((), ()))):
    return lax.dot_general(a, b, dims, preferred_element_type=f32)


def two_parts(value):
    high = value.astype(bf16)
    low = (value - high.astype(f32)).astype(bf16)
    return jnp.concatenate([high, low], axis=1)


def halves(own, other, half):
    own, other = own.astype(f32), other.astype(f32)
    first = jnp.where(half == 0, own, other)
    second = jnp.where(half == 0, other, own)
    return jnp.concatenate([first, second], axis=0).astype(bf16)


def place_of(shard, half, count):
    return jnp.bitwise_xor(shard, half * (count // 2))


def whole_call(body, args, shapes, scratch=(), flops=0, moved=0, limit=12 << 20):
    one = pl.BlockSpec(memory_space=pltpu.VMEM)
    return pl.pallas_call(
        body,
        in_specs=[one] * len(args),
        out_specs=[one] * len(shapes),
        out_shape=shapes,
        scratch_shapes=scratch,
        compiler_params=pltpu.CompilerParams(vmem_limit_bytes=limit),
        cost_estimate=pl.CostEstimate(flops=flops, bytes_accessed=moved, transcendentals=0),
    )(*args)


def in_hbm(array):
    return pltpu.with_memory_space_constraint(array, pltpu.HBM)


def shaped(shape, dtype):
    return jax.ShapeDtypeStruct(shape, dtype)


def choose_kernel(returned, head, out):
    slot = lax.axis_index("section")
    width = out.shape[1]
    spot = pl.ds(pl.multiple_of((slot % 2) * width, width), width)

    @pl.when(slot < 2)
    def _():
        pltpu.sync_copy(head.at[:, spot], out)

    @pl.when(slot >= 2)
    def _():
        pltpu.sync_copy(returned, out)


def choose(returned, head):
    return pl.pallas_call(
        choose_kernel,
        in_specs=[pl.BlockSpec(memory_space=pltpu.HBM)] * 2,
        out_specs=pl.BlockSpec(memory_space=pltpu.VMEM),
        out_shape=shaped(returned.shape, bf16),
        name="choose",
        compiler_params=pltpu.CompilerParams(vmem_limit_bytes=4 << 20),
    )(in_hbm(returned), in_hbm(head))


def forward_kernel(count, rows, nb, xo, xt, yo, yt, ao, at, b_in, w_in, *refs):
    outs, (pack, w, ys, fac, b) = refs[:count], refs[count : count + 5]
    xs, res, a_first, a_second, sems = refs[count + 5 :]
    half = lax.axis_index("section") % 2
    me = lax.axis_index("tensor")
    ht = xo.shape[0]
    tokens = 2 * ht
    rank, width = b.shape
    lines, across = pack.shape[0] - rank, pack.shape[1]
    cuts = [pl.ds(j, nb) for j in range(0, width, nb)]
    moves = [
        (ao, a_first),
        (at, a_second),
        (b_in, b),
        (xo, xs.at[:ht, :]),
        (xt, xs.at[ht:tokens, :]),
        (w_in.at[:, cuts[0]], w.at[:, cuts[0]]),
        (yo, ys.at[:ht, :]),
        (yt, ys.at[ht:, :]),
    ] + [(w_in.at[:, c], w.at[:, c]) for c in cuts[1:]]
    copies = [pltpu.make_async_copy(m[0], m[1], sems.at[i]) for i, m in enumerate(moves)]
    for copy in copies:
        copy.start()
    for copy in copies[:5]:
        copy.wait()
    fac[...] = halves(a_first[...], a_second[...], half)
    xs[tokens:, :] = fac[...]
    lx = two_parts(dot(xs[:tokens, :], fac[...], NT))
    gram = two_parts(dot(fac[...], fac[...], NT))
    for n, j in enumerate(range(0, width, nb)):
        copies[5 if n == 0 else 7 + n].wait()
        cut = slice(j, j + nb)
        wv, bv = w[:, cut], b[:, cut]
        both_b = jnp.concatenate([bv, bv], axis=0)
        total = dot(xs[...], wv)
        res[...] = total[:tokens] + dot(lx, both_b)
        wf = wv.astype(f32)
        squares = jnp.sum((wf * wf).reshape(wf.shape[0] // 8, 8, nb), axis=0)
        cross = 2.0 * total[tokens:] + dot(gram, both_b)
        cross = bv.astype(f32) * cross
        for r in range(0, rank, 8):
            squares = squares + cross[r : r + 8]
        squares = jnp.sum(squares, axis=0, keepdims=True)
        for i in range(0, nb, across):
            at_line = (j + i) // across
            pack[at_line : at_line + 1, :] = squares[:, i : i + across]
        for k in range(count):
            at_row = place_of(jnp.bitwise_xor(me, k), half, count) * rows
            piece = res[pl.ds(pl.multiple_of(at_row, rows), rows), :]
            outs[k][:, cut] = piece.astype(outs[k].dtype)
        if n == 0:
            copies[6].wait()
            copies[7].wait()
            pack[lines:, :] = dot(ys[...], fac[...], NT).T


def forward(count, rows, xo, xt, yo, yt, ao, at, b, w):
    ff, width = w.shape
    ht = xo.shape[0]
    tokens = 2 * ht
    rank = b.shape[0]
    nb = block_of(width, 512)
    args = (in_hbm(xo), xt, in_hbm(yo), yt, in_hbm(ao), at, in_hbm(b), in_hbm(w))
    shapes = [shaped((rows, width), f32 if k == 0 else bf16) for k in range(count)] + [
        shaped((width // tokens + rank, tokens), f32),
        shaped(w.shape, bf16),
        shaped((tokens, ff), bf16),
        shaped((rank, ff), bf16),
        shaped(b.shape, bf16),
    ]
    return pl.pallas_call(
        functools.partial(forward_kernel, count, rows, nb),
        in_specs=[pl.BlockSpec(memory_space=m) for m in (pltpu.HBM, pl.ANY) * 3 + (pltpu.HBM,) * 2],
        out_specs=[pl.BlockSpec(memory_space=pltpu.VMEM)] * len(shapes),
        out_shape=shapes,
        scratch_shapes=[
            pltpu.VMEM((tokens + rank, ff), bf16),
            pltpu.VMEM((tokens, nb), f32),
            pltpu.VMEM((rank // 2, ff), bf16),
            pltpu.VMEM((rank // 2, ff), bf16),
            pltpu.SemaphoreType.DMA((7 + width // nb,)),
        ],
        name="forward",
        compiler_params=pltpu.CompilerParams(vmem_limit_bytes=12 << 20),
        cost_estimate=pl.CostEstimate(
            flops=2 * tokens * ff * width, bytes_accessed=2 * ff * width, transcendentals=0
        ),
    )(*args)


def again_kernel(nb, ys, pack, b, w, out):
    rank, width = b.shape
    ly = two_parts(pack[pack.shape[0] - rank :, :].T)
    for j in range(0, width, nb):
        cut = slice(j, j + nb)
        both_b = jnp.concatenate([b[:, cut], b[:, cut]], axis=0)
        out[:, cut] = dot(ys[...], w[:, cut]) + dot(ly, both_b)


def again(ys, pack, b, w):
    ff, width = w.shape
    tokens = ys.shape[0]
    return whole_call(
        functools.partial(again_kernel, block_of(width, 512)),
        (ys, pack, b, w),
        [shaped((tokens, width), f32)],
        (),
        2 * tokens * ff * width,
        2 * ff * width,
    )[0]


def backward_kernel(count, rows, rb, *refs):
    cots, packs = refs[:count], refs[count : 2 * count]
    mag, r, b, fac, w = refs[2 * count : 2 * count + 5]
    own, send, adapt, gb, magpack, norms = refs[2 * count + 5 : 2 * count + 11]
    (sc,) = refs[2 * count + 11 :]
    half = lax.axis_index("section") % 2
    me = lax.axis_index("tensor")
    rank = b.shape[0]
    tokens, width = sc.shape
    total = packs[0][...]
    for k in range(1, count):
        total = total + packs[k][...]
    lines = total.shape[0] - rank
    across = total.shape[1]
    sqr = jnp.sqrt(jnp.maximum(total[:lines], 0.0) + epsilon)
    for i in range(lines):
        norms[0:1, i * across : (i + 1) * across] = sqr[i : i + 1, :]
    scale = mag[...] / norms[0:1, :]
    norms[1:2, :] = scale
    mags = jnp.zeros((8, width), f32)
    for k in range(count):
        at_row = place_of(jnp.bitwise_xor(me, k), half, count) * rows
        spot = pl.ds(pl.multiple_of(at_row, rows), rows)
        cot = cots[k][...].astype(f32)
        sc[spot, :] = (cot * scale).astype(bf16)
        mags = mags + jnp.sum((cot * r[spot, :]).reshape(rows // 8, 8, width), axis=0)
    mags = jnp.sum(mags, axis=0, keepdims=True)
    for i in range(lines):
        magpack[i : i + 1, :] = mags[:, i * across : (i + 1) * across]
    part = dot(sc[...], b[...], NT)
    adapt[...] = part
    ad = two_parts(part)
    gb[...] = dot(total[lines:].astype(bf16), sc[...])
    for j in range(0, w.shape[0], rb):
        cut = slice(j, j + rb)
        both_a = jnp.concatenate([fac[:, cut], fac[:, cut]], axis=0)
        out = dot(sc[...], w[cut, :], NT) + dot(ad, both_a)
        own[:, cut] = out[: tokens // 2]
        send[:, cut] = out[tokens // 2 :].astype(bf16)


def backward(count, rows, cots, packs, mag, r, b, fac, w):
    ff, width = w.shape
    tokens = rows * count
    rank = b.shape[0]
    return whole_call(
        functools.partial(backward_kernel, count, rows, block_of(ff, 512)),
        (*cots, *packs, mag, r, b, fac, w),
        [
            shaped((tokens // 2, ff), f32),
            shaped((tokens // 2, ff), bf16),
            shaped((tokens, rank), f32),
            shaped((rank, width), f32),
            shaped((width // tokens, tokens), f32),
            shaped((2, width), f32),
        ],
        [pltpu.VMEM((tokens, width), bf16)],
        2 * tokens * ff * width,
        2 * ff * width,
    )


def emit_kernel(count, *refs):
    parts = refs[:count]
    carried, embedded, norms, out = refs[count:]
    slot = lax.axis_index("section")
    half = slot % 2
    width = out.shape[1]
    here = embedded[:, pl.ds(pl.multiple_of(half * width, width), width)].astype(f32)
    inflow = jnp.where(slot < 2, here, carried[...].astype(f32))
    total = parts[0][...]
    for k in range(1, count):
        total = total + parts[k][...].astype(f32)
    out[...] = (inflow + total * norms[1:2, :]).astype(bf16)


def emit(count, parts, carried, embedded, norms):
    return whole_call(
        functools.partial(emit_kernel, count),
        (*parts, carried, embedded, norms),
        [shaped(carried.shape, bf16)],
        moved=8 * carried.size * 2,
    )[0]


def finish_kernel(count, *refs):
    own, got, adapt, got_adapt, ys = refs[:5]
    mags = refs[5 : 5 + count]
    norms = refs[5 + count]
    hidden, ga, gm = refs[6 + count :]
    half = lax.axis_index("section") % 2
    hidden[...] = (own[...] + got[...].astype(f32)).astype(bf16)
    tokens, rank = adapt.shape
    ht, hr = tokens // 2, rank // 2
    first = adapt[:ht, :] + got_adapt[ht:, :]
    second = adapt[ht:, :] + got_adapt[:ht, :]
    pick = lambda v: jnp.where(half == 0, v[:, :hr], v[:, hr:]).astype(bf16)
    ga[...] = dot(pick(jnp.concatenate([first, second], axis=0)), ys[...], TN)
    total = mags[0][...]
    for k in range(1, count):
        total = total + mags[k][...]
    across = total.shape[1]
    for i in range(total.shape[0]):
        cut = slice(i * across, (i + 1) * across)
        gm[:, cut] = total[i : i + 1, :] / norms[0:1, cut]


def finish(count, own, got, adapt, got_adapt, ys, mags, norms):
    ht, ff = own.shape
    rank = adapt.shape[1]
    return whole_call(
        functools.partial(finish_kernel, count),
        (own, got, adapt, got_adapt, ys, *mags, norms),
        [shaped((ht, ff), bf16), shaped((rank // 2, ff), f32), shaped((1, norms.shape[1]), f32)],
        moved=12 * ht * ff,
    )


def local(
    frozen,
    adapter_a,
    adapter_b,
    magnitude,
    hidden_fwd,
    carried,
    embedded,
    hidden_bwd,
    returned,
    head_grad,
):
    w, ao, b, xo, yo = frozen[0], adapter_a[0], adapter_b[0], hidden_fwd[0], hidden_bwd[0]
    slots = lax.axis_size("section")
    count = lax.axis_size("tensor")
    rows = carried.shape[1]

    def swap(array):
        return lax.ppermute(array, "section", [(i, i ^ 1) for i in range(slots)])

    def across(array, k):
        return lax.ppermute(array, "tensor", [(i, i ^ k) for i in range(count)])

    def shift(array, k):
        pairs = [
            (((s + 2) % slots) * count + t, s * count + (t ^ k))
            for s in range(slots)
            for t in range(count)
        ]
        return lax.ppermute(array, ("section", "tensor"), pairs)

    leaving = choose(returned[0], head_grad)
    xt, at, yt = swap(xo), swap(ao), swap(yo)
    cots = [None] * count
    for k in range(0, count, 2):
        cots[k] = shift(leaving, k)
        cots[k + 1] = across(cots[k], 1)
    arriving = lax.ppermute(carried[0], "section", [(i, i + 2) for i in range(slots - 2)])
    *parts, pack, w, ys, fac, b = forward(count, rows, xo, xt, yo, yt, ao, at, b, w)
    packs = [pack]
    for k in range(1, count):
        parts[k] = across(parts[k], k)
    for k in range(1, count):
        packs.append(across(pack, k))
    r = again(ys, pack, b, w)
    own, send, adapt, gb, magpack, norms = backward(
        count, rows, cots, packs, magnitude, r, b, fac, w
    )
    got, got_adapt = swap(send), swap(adapt)
    mags = [magpack]
    for k in range(1, count):
        mags.append(across(magpack, k))
    out = emit(count, parts, arriving, embedded, norms)
    hidden, ga, gm = finish(count, own, got, adapt, got_adapt, ys, mags, norms)
    return (out[None], gm, ga[None], gb[None], hidden[None])


def solution(mesh):
    placed = (
        P("section", "tensor", None),
        P("section", None, "tensor"),
        P("section", None, None),
        P("section", None),
        P("section", None, "tensor"),
        P("section", "tensor", None),
        P("tensor", None),
        P("section", None, "tensor"),
        P("section", "tensor", None),
        P("tensor", None),
    )

    return jax.shard_map(
        local,
        mesh=mesh,
        in_specs=placed,
        out_specs=(
            P("section", "tensor", None),
            P("section", None),
            P("section", None, "tensor"),
            P("section", None, None),
            P("section", None, "tensor"),
        ),
        check_vma=False,
    )
```

```python
import functools

import jax
import jax.numpy as jnp
from jax import lax
from jax.experimental import pallas as pl
from jax.experimental.pallas import tpu as pltpu
from jax.sharding import PartitionSpec as P

epsilon = 1e-06
f32 = jnp.float32
bf16 = jnp.bfloat16
NT = (((1,), (1,)), ((), ()))
TN = (((0,), (0,)), ((), ()))


def block_of(size, most):
    return max(b for b in range(128, most + 1, 128) if size % b == 0)


def dot(a, b, dims=(((1,), (0,)), ((), ()))):
    return lax.dot_general(a, b, dims, preferred_element_type=f32)


def two_parts(value):
    high = value.astype(bf16)
    low = (value - high.astype(f32)).astype(bf16)
    return jnp.concatenate([high, low], axis=1)


def halves(own, other, half):
    own, other = own.astype(f32), other.astype(f32)
    first = jnp.where(half == 0, own, other)
    second = jnp.where(half == 0, other, own)
    return jnp.concatenate([first, second], axis=0).astype(bf16)


def place_of(shard, half, count):
    return jnp.bitwise_xor(shard, half * (count // 2))


def whole_call(body, args, shapes, scratch=(), flops=0, moved=0, limit=12 << 20):
    one = pl.BlockSpec(memory_space=pltpu.VMEM)
    return pl.pallas_call(
        body,
        in_specs=[one] * len(args),
        out_specs=[one] * len(shapes),
        out_shape=shapes,
        scratch_shapes=scratch,
        compiler_params=pltpu.CompilerParams(vmem_limit_bytes=limit),
        cost_estimate=pl.CostEstimate(flops=flops, bytes_accessed=moved, transcendentals=0),
    )(*args)


def in_hbm(array):
    return pltpu.with_memory_space_constraint(array, pltpu.HBM)


def shaped(shape, dtype):
    return jax.ShapeDtypeStruct(shape, dtype)


def choose_kernel(returned, head, out):
    slot = lax.axis_index("section")
    width = out.shape[1]
    spot = pl.ds(pl.multiple_of((slot % 2) * width, width), width)

    @pl.when(slot < 2)
    def _():
        pltpu.sync_copy(head.at[:, spot], out)

    @pl.when(slot >= 2)
    def _():
        pltpu.sync_copy(returned, out)


def choose(returned, head, hidden):
    return pl.pallas_call(
        choose_kernel,
        in_specs=[pl.BlockSpec(memory_space=pltpu.HBM)] * 2,
        out_specs=pl.BlockSpec(memory_space=pltpu.VMEM),
        out_shape=shaped(returned.shape, bf16),
        name="choose",
        compiler_params=pltpu.CompilerParams(vmem_limit_bytes=4 << 20),
        cost_estimate=pl.CostEstimate(
            flops=hidden, bytes_accessed=2 * returned.size, transcendentals=0
        ),
    )(in_hbm(returned), in_hbm(head))


def forward_kernel(count, rows, nb, xo, xt, yo, yt, ao, at, b, w, *refs):
    outs, (pack, ys, fac) = refs[:count], refs[count : count + 3]
    xs, res = refs[count + 3 :]
    half = lax.axis_index("section") % 2
    me = lax.axis_index("tensor")
    ht = xo.shape[0]
    tokens = 2 * ht
    rank, width = b.shape
    lines, across = pack.shape[0] - rank, pack.shape[1]
    fac[...] = halves(ao[...], at[...], half)
    xs[:ht, :] = xo[...]
    xs[ht:tokens, :] = xt[...]
    xs[tokens:, :] = fac[...]
    ys[:ht, :] = yo[...]
    ys[ht:, :] = yt[...]
    lx = two_parts(dot(xs[:tokens, :], fac[...], NT))
    gram = two_parts(dot(fac[...], fac[...], NT))
    pack[lines:, :] = dot(ys[...], fac[...], NT).T
    for j in range(0, width, nb):
        cut = slice(j, j + nb)
        wv, bv = w[:, cut], b[:, cut]
        both_b = jnp.concatenate([bv, bv], axis=0)
        total = dot(xs[...], wv)
        res[...] = total[:tokens] + dot(lx, both_b)
        wf = wv.astype(f32)
        squares = jnp.sum((wf * wf).reshape(wf.shape[0] // 8, 8, nb), axis=0)
        cross = 2.0 * total[tokens:] + dot(gram, both_b)
        cross = bv.astype(f32) * cross
        for r in range(0, rank, 8):
            squares = squares + cross[r : r + 8]
        squares = jnp.sum(squares, axis=0, keepdims=True)
        for i in range(0, nb, across):
            at_line = (j + i) // across
            pack[at_line : at_line + 1, :] = squares[:, i : i + across]
        for k in range(count):
            at_row = place_of(jnp.bitwise_xor(me, k), half, count) * rows
            piece = res[pl.ds(pl.multiple_of(at_row, rows), rows), :]
            outs[k][:, cut] = piece.astype(outs[k].dtype)


def forward(count, rows, xo, xt, yo, yt, ao, at, b, w):
    ff, width = w.shape
    tokens = 2 * xo.shape[0]
    rank = b.shape[0]
    nb = block_of(width, 512)
    return whole_call(
        functools.partial(forward_kernel, count, rows, nb),
        (xo, xt, yo, yt, ao, at, b, w),
        [shaped((rows, width), f32 if k == 0 else bf16) for k in range(count)]
        + [
            shaped((width // tokens + rank, tokens), f32),
            shaped((tokens, ff), bf16),
            shaped((rank, ff), bf16),
        ],
        [pltpu.VMEM((tokens + rank, ff), bf16), pltpu.VMEM((tokens, nb), f32)],
        2 * tokens * ff * width,
        2 * ff * width,
    )


def again_kernel(nb, ys, pack, b, w, out):
    rank, width = b.shape
    ly = two_parts(pack[pack.shape[0] - rank :, :].T)
    for j in range(0, width, nb):
        cut = slice(j, j + nb)
        both_b = jnp.concatenate([b[:, cut], b[:, cut]], axis=0)
        out[:, cut] = dot(ys[...], w[:, cut]) + dot(ly, both_b)


def again(ys, pack, b, w):
    ff, width = w.shape
    tokens = ys.shape[0]
    return whole_call(
        functools.partial(again_kernel, block_of(width, 512)),
        (ys, pack, b, w),
        [shaped((tokens, width), f32)],
        (),
        2 * tokens * ff * width,
        2 * ff * width,
    )[0]


def join_kernel(one, two, out):
    out[...] = one[...] + two[...]


def join(one, two):
    return whole_call(join_kernel, (one, two), [shaped(one.shape, f32)])[0]


def prepare_kernel(count, rows, *refs):
    cots = refs[:count]
    packs, mag, r, b = refs[count : count + 2], *refs[count + 2 : count + 5]
    sc, ad, adapt, gb, magpack, norms = refs[count + 5 :]
    half = lax.axis_index("section") % 2
    me = lax.axis_index("tensor")
    rank = b.shape[0]
    _, width = sc.shape
    total = packs[0][...] + packs[1][...]
    lines = total.shape[0] - rank
    across = total.shape[1]
    sqr = jnp.sqrt(jnp.maximum(total[:lines], 0.0) + epsilon)
    for i in range(lines):
        norms[0:1, i * across : (i + 1) * across] = sqr[i : i + 1, :]
    scale = mag[...] / norms[0:1, :]
    norms[1:2, :] = scale
    mags = jnp.zeros((8, width), f32)
    for k in range(count):
        at_row = place_of(jnp.bitwise_xor(me, k), half, count) * rows
        spot = pl.ds(pl.multiple_of(at_row, rows), rows)
        cot = cots[k][...].astype(f32)
        sc[spot, :] = (cot * scale).astype(bf16)
        mags = mags + jnp.sum((cot * r[spot, :]).reshape(rows // 8, 8, width), axis=0)
    mags = jnp.sum(mags, axis=0, keepdims=True)
    for i in range(lines):
        magpack[i : i + 1, :] = mags[:, i * across : (i + 1) * across]
    part = dot(sc[...], b[...], NT)
    adapt[...] = part
    ad[...] = two_parts(part)
    gb[...] = dot(total[lines:].astype(bf16), sc[...])


def prepare(count, rows, cots, packs, mag, r, b):
    width = b.shape[1]
    tokens = rows * count
    rank = b.shape[0]
    return whole_call(
        functools.partial(prepare_kernel, count, rows),
        (*cots, *packs, mag, r, b),
        [
            shaped((tokens, width), bf16),
            shaped((tokens, 2 * rank), bf16),
            shaped((tokens, rank), f32),
            shaped((rank, width), f32),
            shaped((width // tokens, tokens), f32),
            shaped((2, width), f32),
        ],
        moved=8 * tokens * width,
    )


def backward_kernel(rb, sc, ad, fac, w, own, send):
    half_tokens = own.shape[0]
    for j in range(0, w.shape[0], rb):
        cut = slice(j, j + rb)
        both_a = jnp.concatenate([fac[:, cut], fac[:, cut]], axis=0)
        out = dot(sc[...], w[cut, :], NT) + dot(ad[...], both_a)
        own[:, cut] = out[:half_tokens]
        send[:, cut] = out[half_tokens:].astype(bf16)


def backward(sc, ad, fac, w):
    ff, width = w.shape
    tokens = sc.shape[0]
    return whole_call(
        functools.partial(backward_kernel, block_of(ff, 512)),
        (sc, ad, fac, w),
        [shaped((tokens // 2, ff), f32), shaped((tokens // 2, ff), bf16)],
        (),
        2 * tokens * ff * width,
        2 * ff * width,
    )


def emit_kernel(count, *refs):
    parts = refs[:count]
    carried, embedded, norms, adapt, got_adapt, ys, out, ga = refs[count:]
    slot = lax.axis_index("section")
    half = slot % 2
    width = out.shape[1]
    here = embedded[:, pl.ds(pl.multiple_of(half * width, width), width)].astype(f32)
    inflow = jnp.where(slot < 2, here, carried[...].astype(f32))
    total = parts[0][...]
    for k in range(1, count):
        total = total + parts[k][...].astype(f32)
    out[...] = (inflow + total * norms[1:2, :]).astype(bf16)
    tokens, rank = adapt.shape
    ht, hr = tokens // 2, rank // 2
    first = adapt[:ht, :] + got_adapt[ht:, :]
    second = adapt[ht:, :] + got_adapt[:ht, :]
    cot = jnp.concatenate([first, second], axis=0)
    cot = jnp.where(half == 0, cot[:, :hr], cot[:, hr:]).astype(bf16)
    ga[...] = dot(cot, ys[...], TN)


def emit(count, parts, carried, embedded, norms, adapt, got_adapt, ys):
    return whole_call(
        functools.partial(emit_kernel, count),
        (*parts, carried, embedded, norms, adapt, got_adapt, ys),
        [shaped(carried.shape, bf16), shaped((adapt.shape[1] // 2, ys.shape[1]), f32)],
        moved=8 * carried.size * 2,
    )


def finish_kernel(count, *refs):
    own, got = refs[:2]
    mags = refs[2 : 2 + count]
    norms = refs[2 + count]
    hidden, gm = refs[3 + count :]
    hidden[...] = (own[...] + got[...].astype(f32)).astype(bf16)
    total = mags[0][...]
    for k in range(1, count):
        total = total + mags[k][...]
    across = total.shape[1]
    for i in range(total.shape[0]):
        cut = slice(i * across, (i + 1) * across)
        gm[:, cut] = total[i : i + 1, :] / norms[0:1, cut]


def finish(count, own, got, mags, norms):
    return whole_call(
        functools.partial(finish_kernel, count),
        (own, got, *mags, norms),
        [shaped(own.shape, bf16), shaped((1, norms.shape[1]), f32)],
        moved=12 * own.size,
    )


def local(
    frozen,
    adapter_a,
    adapter_b,
    magnitude,
    hidden_fwd,
    carried,
    embedded,
    hidden_bwd,
    returned,
    head_grad,
):
    w, ao, b, xo, yo = frozen[0], adapter_a[0], adapter_b[0], hidden_fwd[0], hidden_bwd[0]
    slots = lax.axis_size("section")
    count = lax.axis_size("tensor")
    rows = carried.shape[1]

    def swap(array):
        return lax.ppermute(array, "section", [(i, i ^ 1) for i in range(slots)])

    def across(array, k):
        return lax.ppermute(array, "tensor", [(i, i ^ k) for i in range(count)])

    def shift(array, k):
        pairs = [
            (((s + 2) % slots) * count + t, s * count + (t ^ k))
            for s in range(slots)
            for t in range(count)
        ]
        return lax.ppermute(array, ("section", "tensor"), pairs)

    leaving = choose(returned[0], head_grad, 4 * rows * count * w.size)
    xt, at, yt = swap(xo), swap(ao), swap(yo)
    cots = [None] * count
    for k in range(count):
        direct = k < 2 or k % 2 == 0
        cots[k] = shift(leaving, k) if direct else across(cots[k - 1], 1)
    arriving = lax.ppermute(carried[0], "section", [(i, (i + 2) % slots) for i in range(slots)])
    *parts, pack, ys, fac = forward(count, rows, xo, xt, yo, yt, ao, at, b, w)
    for k in range(1, count):
        parts[k] = across(parts[k], k)
    got = across(pack, 1)
    r = again(ys, pack, b, w)
    for k in (2**n for n in range(1, count.bit_length() - 1)):
        pack = join(pack, got)
        got = across(pack, k)
    sc, ad, adapt, gb, magpack, norms = prepare(
        count, rows, cots, (pack, got), magnitude, r, b
    )
    got_adapt = swap(adapt)
    mags = [magpack]
    for k in range(1, count):
        mags.append(across(magpack, k))
    own, send = backward(sc, ad, fac, w)
    got = swap(send)
    out, ga = emit(count, parts, arriving, embedded, norms, adapt, got_adapt, ys)
    hidden, gm = finish(count, own, got, mags, norms)
    return (out[None], gm, ga[None], gb[None], hidden[None])


def solution(mesh):
    placed = (
        P("section", "tensor", None),
        P("section", None, "tensor"),
        P("section", None, None),
        P("section", None),
        P("section", None, "tensor"),
        P("section", "tensor", None),
        P("tensor", None),
        P("section", None, "tensor"),
        P("section", "tensor", None),
        P("tensor", None),
    )

    return jax.shard_map(
        local,
        mesh=mesh,
        in_specs=placed,
        out_specs=(
            P("section", "tensor", None),
            P("section", None),
            P("section", None, "tensor"),
            P("section", None, None),
            P("section", None, "tensor"),
        ),
        check_vma=False,
    )
```

```python
import functools

import jax
import jax.numpy as jnp
from jax import lax
from jax.experimental import pallas as pl
from jax.experimental.pallas import tpu as pltpu
from jax.sharding import PartitionSpec as P

epsilon = 1e-06
f32 = jnp.float32
bf16 = jnp.bfloat16
NT = (((1,), (1,)), ((), ()))
TN = (((0,), (0,)), ((), ()))


def block_of(size, most):
    return max(b for b in range(128, most + 1, 128) if size % b == 0)


def dot(a, b, dims=(((1,), (0,)), ((), ()))):
    return lax.dot_general(a, b, dims, preferred_element_type=f32)


def two_parts(value):
    high = value.astype(bf16)
    low = (value - high.astype(f32)).astype(bf16)
    return jnp.concatenate([high, low], axis=1)


def halves(own, other, half):
    own, other = own.astype(f32), other.astype(f32)
    first = jnp.where(half == 0, own, other)
    second = jnp.where(half == 0, other, own)
    return jnp.concatenate([first, second], axis=0).astype(bf16)


def place_of(shard, half, count):
    return jnp.bitwise_xor(shard, half * (count // 2))


def whole_call(body, args, shapes, scratch=(), flops=0, moved=0, limit=12 << 20):
    one = pl.BlockSpec(memory_space=pltpu.VMEM)
    return pl.pallas_call(
        body,
        in_specs=[one] * len(args),
        out_specs=[one] * len(shapes),
        out_shape=shapes,
        scratch_shapes=scratch,
        compiler_params=pltpu.CompilerParams(vmem_limit_bytes=limit),
        cost_estimate=pl.CostEstimate(flops=flops, bytes_accessed=moved, transcendentals=0),
    )(*args)


def in_hbm(array):
    return pltpu.with_memory_space_constraint(array, pltpu.HBM)


def shaped(shape, dtype):
    return jax.ShapeDtypeStruct(shape, dtype)


def choose_kernel(returned, head, out):
    slot = lax.axis_index("section")
    width = out.shape[1]
    spot = pl.ds(pl.multiple_of((slot % 2) * width, width), width)

    @pl.when(slot < 2)
    def _():
        pltpu.sync_copy(head.at[:, spot], out)

    @pl.when(slot >= 2)
    def _():
        pltpu.sync_copy(returned, out)


def choose(returned, head, hidden):
    return pl.pallas_call(
        choose_kernel,
        in_specs=[pl.BlockSpec(memory_space=pltpu.HBM)] * 2,
        out_specs=pl.BlockSpec(memory_space=pltpu.VMEM),
        out_shape=shaped(returned.shape, bf16),
        name="choose",
        compiler_params=pltpu.CompilerParams(vmem_limit_bytes=4 << 20),
        cost_estimate=pl.CostEstimate(
            flops=hidden, bytes_accessed=2 * returned.size, transcendentals=0
        ),
    )(in_hbm(returned), in_hbm(head))


def forward_kernel(count, rows, nb, xo, xt, yo, yt, ao, at, b, w, *refs):
    outs, (pack, ys, fac) = refs[:count], refs[count : count + 3]
    xs, res = refs[count + 3 :]
    half = lax.axis_index("section") % 2
    me = lax.axis_index("tensor")
    ht = xo.shape[0]
    tokens = 2 * ht
    rank, width = b.shape
    lines, across = pack.shape[0] - rank, pack.shape[1]
    fac[...] = halves(ao[...], at[...], half)
    xs[:ht, :] = xo[...]
    xs[ht:tokens, :] = xt[...]
    xs[tokens:, :] = fac[...]
    ys[:ht, :] = yo[...]
    ys[ht:, :] = yt[...]
    lx = two_parts(dot(xs[:tokens, :], fac[...], NT))
    gram = two_parts(dot(fac[...], fac[...], NT))
    pack[lines:, :] = dot(ys[...], fac[...], NT).T
    for j in range(0, width, nb):
        cut = slice(j, j + nb)
        wv, bv = w[:, cut], b[:, cut]
        both_b = jnp.concatenate([bv, bv], axis=0)
        total = dot(xs[...], wv)
        res[...] = total[:tokens] + dot(lx, both_b)
        wf = wv.astype(f32)
        squares = jnp.sum((wf * wf).reshape(wf.shape[0] // 8, 8, nb), axis=0)
        cross = 2.0 * total[tokens:] + dot(gram, both_b)
        cross = bv.astype(f32) * cross
        for r in range(0, rank, 8):
            squares = squares + cross[r : r + 8]
        squares = jnp.sum(squares, axis=0, keepdims=True)
        for i in range(0, nb, across):
            at_line = (j + i) // across
            pack[at_line : at_line + 1, :] = squares[:, i : i + across]
        for k in range(count):
            at_row = place_of(jnp.bitwise_xor(me, k), half, count) * rows
            piece = res[pl.ds(pl.multiple_of(at_row, rows), rows), :]
            outs[k][:, cut] = piece.astype(outs[k].dtype)


def forward(count, rows, xo, xt, yo, yt, ao, at, b, w):
    ff, width = w.shape
    tokens = 2 * xo.shape[0]
    rank = b.shape[0]
    nb = block_of(width, 512)
    return whole_call(
        functools.partial(forward_kernel, count, rows, nb),
        (xo, xt, yo, yt, ao, at, b, w),
        [shaped((rows, width), f32 if k == 0 else bf16) for k in range(count)]
        + [
            shaped((width // tokens + rank, tokens), f32),
            shaped((tokens, ff), bf16),
            shaped((rank, ff), bf16),
        ],
        [pltpu.VMEM((tokens + rank, ff), bf16), pltpu.VMEM((tokens, nb), f32)],
        2 * tokens * ff * width,
        2 * ff * width,
    )


def again_kernel(nb, ys, pack, b, w, out):
    rank, width = b.shape
    ly = two_parts(pack[pack.shape[0] - rank :, :].T)
    for j in range(0, width, nb):
        cut = slice(j, j + nb)
        both_b = jnp.concatenate([b[:, cut], b[:, cut]], axis=0)
        out[:, cut] = dot(ys[...], w[:, cut]) + dot(ly, both_b)


def again(ys, pack, b, w):
    ff, width = w.shape
    tokens = ys.shape[0]
    return whole_call(
        functools.partial(again_kernel, block_of(width, 512)),
        (ys, pack, b, w),
        [shaped((tokens, width), f32)],
        (),
        2 * tokens * ff * width,
        2 * ff * width,
    )[0]


def join_kernel(one, two, out):
    out[...] = one[...] + two[...]


def join(one, two):
    return whole_call(join_kernel, (one, two), [shaped(one.shape, f32)])[0]


def prepare_kernel(count, rows, *refs):
    cots = refs[:count]
    packs, mag, r, b = refs[count : count + 2], *refs[count + 2 : count + 5]
    sc, ad, adapt, low, magpack, norms = refs[count + 5 :]
    half = lax.axis_index("section") % 2
    me = lax.axis_index("tensor")
    rank = b.shape[0]
    _, width = sc.shape
    total = packs[0][...] + packs[1][...]
    lines = total.shape[0] - rank
    across = total.shape[1]
    sqr = jnp.sqrt(jnp.maximum(total[:lines], 0.0) + epsilon)
    for i in range(lines):
        norms[0:1, i * across : (i + 1) * across] = sqr[i : i + 1, :]
    scale = mag[...] / norms[0:1, :]
    norms[1:2, :] = scale
    mags = jnp.zeros((8, width), f32)
    for k in range(count):
        at_row = place_of(jnp.bitwise_xor(me, k), half, count) * rows
        spot = pl.ds(pl.multiple_of(at_row, rows), rows)
        cot = cots[k][...].astype(f32)
        sc[spot, :] = (cot * scale).astype(bf16)
        mags = mags + jnp.sum((cot * r[spot, :]).reshape(rows // 8, 8, width), axis=0)
    mags = jnp.sum(mags, axis=0, keepdims=True)
    for i in range(lines):
        magpack[i : i + 1, :] = mags[:, i * across : (i + 1) * across]
    part = dot(sc[...], b[...], NT)
    adapt[...] = part
    ad[...] = two_parts(part)
    low[...] = total[lines:].astype(bf16)


def prepare(count, rows, cots, packs, mag, r, b):
    width = b.shape[1]
    tokens = rows * count
    rank = b.shape[0]
    return whole_call(
        functools.partial(prepare_kernel, count, rows),
        (*cots, *packs, mag, r, b),
        [
            shaped((tokens, width), bf16),
            shaped((tokens, 2 * rank), bf16),
            shaped((tokens, rank), f32),
            shaped((rank, tokens), bf16),
            shaped((width // tokens, tokens), f32),
            shaped((2, width), f32),
        ],
        moved=8 * tokens * width,
    )


def backward_kernel(rb, sc, ad, fac, w, own, send):
    half_tokens = own.shape[0]
    for j in range(0, w.shape[0], rb):
        cut = slice(j, j + rb)
        both_a = jnp.concatenate([fac[:, cut], fac[:, cut]], axis=0)
        out = dot(sc[...], w[cut, :], NT) + dot(ad[...], both_a)
        own[:, cut] = out[:half_tokens]
        send[:, cut] = out[half_tokens:].astype(bf16)


def backward(sc, ad, fac, w):
    ff, width = w.shape
    tokens = sc.shape[0]
    return whole_call(
        functools.partial(backward_kernel, block_of(ff, 512)),
        (sc, ad, fac, w),
        [shaped((tokens // 2, ff), f32), shaped((tokens // 2, ff), bf16)],
        (),
        2 * tokens * ff * width,
        2 * ff * width,
    )


def emit_kernel(count, *refs):
    parts = refs[:count]
    carried, embedded, norms, adapt, got_adapt, ys, low, sc, out, ga, gb = refs[count:]
    slot = lax.axis_index("section")
    half = slot % 2
    width = out.shape[1]
    here = embedded[:, pl.ds(pl.multiple_of(half * width, width), width)].astype(f32)
    inflow = jnp.where(slot < 2, here, carried[...].astype(f32))
    total = parts[0][...]
    for k in range(1, count):
        total = total + parts[k][...].astype(f32)
    out[...] = (inflow + total * norms[1:2, :]).astype(bf16)
    tokens, rank = adapt.shape
    ht, hr = tokens // 2, rank // 2
    first = adapt[:ht, :] + got_adapt[ht:, :]
    second = adapt[ht:, :] + got_adapt[:ht, :]
    cot = jnp.concatenate([first, second], axis=0)
    cot = jnp.where(half == 0, cot[:, :hr], cot[:, hr:]).astype(bf16)
    ga[...] = dot(cot, ys[...], TN)
    gb[...] = dot(low[...], sc[...])


def emit(count, parts, carried, embedded, norms, adapt, got_adapt, ys, low, sc):
    return whole_call(
        functools.partial(emit_kernel, count),
        (*parts, carried, embedded, norms, adapt, got_adapt, ys, low, sc),
        [
            shaped(carried.shape, bf16),
            shaped((adapt.shape[1] // 2, ys.shape[1]), f32),
            shaped((adapt.shape[1], sc.shape[1]), f32),
        ],
        moved=8 * carried.size * 2,
    )


def finish_kernel(count, *refs):
    own, got = refs[:2]
    mags = refs[2 : 2 + count]
    norms = refs[2 + count]
    hidden, gm = refs[3 + count :]
    hidden[...] = (own[...] + got[...].astype(f32)).astype(bf16)
    total = mags[0][...]
    for k in range(1, count):
        total = total + mags[k][...]
    across = total.shape[1]
    for i in range(total.shape[0]):
        cut = slice(i * across, (i + 1) * across)
        gm[:, cut] = total[i : i + 1, :] / norms[0:1, cut]


def finish(count, own, got, mags, norms):
    return whole_call(
        functools.partial(finish_kernel, count),
        (own, got, *mags, norms),
        [shaped(own.shape, bf16), shaped((1, norms.shape[1]), f32)],
        moved=12 * own.size,
    )


def local(
    frozen,
    adapter_a,
    adapter_b,
    magnitude,
    hidden_fwd,
    carried,
    embedded,
    hidden_bwd,
    returned,
    head_grad,
):
    w, ao, b, xo, yo = frozen[0], adapter_a[0], adapter_b[0], hidden_fwd[0], hidden_bwd[0]
    slots = lax.axis_size("section")
    count = lax.axis_size("tensor")
    rows = carried.shape[1]

    def swap(array):
        return lax.ppermute(array, "section", [(i, i ^ 1) for i in range(slots)])

    def across(array, k):
        return lax.ppermute(array, "tensor", [(i, i ^ k) for i in range(count)])

    def shift(array, k):
        pairs = [
            (((s + 2) % slots) * count + t, s * count + (t ^ k))
            for s in range(slots)
            for t in range(count)
        ]
        return lax.ppermute(array, ("section", "tensor"), pairs)

    leaving = choose(returned[0], head_grad, 4 * rows * count * w.size)
    xt, at, yt = swap(xo), swap(ao), swap(yo)
    cots = [None] * count
    for k in range(count):
        direct = k < 2 or k % 2 == 0
        cots[k] = shift(leaving, k) if direct else across(cots[k - 1], 1)
    arriving = lax.ppermute(carried[0], "section", [(i, (i + 2) % slots) for i in range(slots)])
    *parts, pack, ys, fac = forward(count, rows, xo, xt, yo, yt, ao, at, b, w)
    for k in range(1, count):
        parts[k] = across(parts[k], k)
    got = across(pack, 1)
    r = again(ys, pack, b, w)
    for k in (2**n for n in range(1, count.bit_length() - 1)):
        pack = join(pack, got)
        got = across(pack, k)
    sc, ad, adapt, low, magpack, norms = prepare(
        count, rows, cots, (pack, got), magnitude, r, b
    )
    got_adapt = swap(adapt)
    mags = [magpack]
    for k in range(1, count):
        mags.append(across(magpack, k))
    own, send = backward(sc, ad, fac, w)
    got = swap(send)
    out, ga, gb = emit(
        count, parts, arriving, embedded, norms, adapt, got_adapt, ys, low, sc
    )
    hidden, gm = finish(count, own, got, mags, norms)
    return (out[None], gm, ga[None], gb[None], hidden[None])


def solution(mesh):
    placed = (
        P("section", "tensor", None),
        P("section", None, "tensor"),
        P("section", None, None),
        P("section", None),
        P("section", None, "tensor"),
        P("section", "tensor", None),
        P("tensor", None),
        P("section", None, "tensor"),
        P("section", "tensor", None),
        P("tensor", None),
    )

    return jax.shard_map(
        local,
        mesh=mesh,
        in_specs=placed,
        out_specs=(
            P("section", "tensor", None),
            P("section", None),
            P("section", None, "tensor"),
            P("section", None, None),
            P("section", None, "tensor"),
        ),
        check_vma=False,
    )
```

```python
import functools

import jax
import jax.numpy as jnp
from jax import lax
from jax.experimental import pallas as pl
from jax.experimental.pallas import tpu as pltpu
from jax.sharding import PartitionSpec as P

epsilon = 1e-06
f32 = jnp.float32
bf16 = jnp.bfloat16
NT = (((1,), (1,)), ((), ()))
TN = (((0,), (0,)), ((), ()))


def block_of(size, most):
    return max(b for b in range(128, most + 1, 128) if size % b == 0)


def dot(a, b, dims=(((1,), (0,)), ((), ()))):
    return lax.dot_general(a, b, dims, preferred_element_type=f32)


def two_parts(value):
    high = value.astype(bf16)
    low = (value - high.astype(f32)).astype(bf16)
    return jnp.concatenate([high, low], axis=1)


def halves(own, other, half):
    own, other = own.astype(f32), other.astype(f32)
    first = jnp.where(half == 0, own, other)
    second = jnp.where(half == 0, other, own)
    return jnp.concatenate([first, second], axis=0).astype(bf16)


def place_of(shard, half, count):
    return jnp.bitwise_xor(shard, half * (count // 2))


def whole_call(body, args, shapes, scratch=(), flops=0, moved=0, limit=12 << 20):
    one = pl.BlockSpec(memory_space=pltpu.VMEM)
    return pl.pallas_call(
        body,
        in_specs=[one] * len(args),
        out_specs=[one] * len(shapes),
        out_shape=shapes,
        scratch_shapes=scratch,
        compiler_params=pltpu.CompilerParams(vmem_limit_bytes=limit),
        cost_estimate=pl.CostEstimate(flops=flops, bytes_accessed=moved, transcendentals=0),
    )(*args)


def in_hbm(array):
    return pltpu.with_memory_space_constraint(array, pltpu.HBM)


def shaped(shape, dtype):
    return jax.ShapeDtypeStruct(shape, dtype)


def choose_kernel(returned, head, out):
    slot = lax.axis_index("section")
    width = out.shape[1]
    spot = pl.ds(pl.multiple_of((slot % 2) * width, width), width)

    @pl.when(slot < 2)
    def _():
        pltpu.sync_copy(head.at[:, spot], out)

    @pl.when(slot >= 2)
    def _():
        pltpu.sync_copy(returned, out)


def choose(returned, head, hidden):
    return pl.pallas_call(
        choose_kernel,
        in_specs=[pl.BlockSpec(memory_space=pltpu.HBM)] * 2,
        out_specs=pl.BlockSpec(memory_space=pltpu.VMEM),
        out_shape=shaped(returned.shape, bf16),
        name="choose",
        compiler_params=pltpu.CompilerParams(vmem_limit_bytes=4 << 20),
        cost_estimate=pl.CostEstimate(
            flops=hidden, bytes_accessed=2 * returned.size, transcendentals=0
        ),
    )(in_hbm(returned), in_hbm(head))


def forward_kernel(count, rows, nb, xo, xt, yo, yt, ao, at, b, w, *refs):
    outs, (pack, ys, fac) = refs[:count], refs[count : count + 3]
    xs, res = refs[count + 3 :]
    half = lax.axis_index("section") % 2
    me = lax.axis_index("tensor")
    ht = xo.shape[0]
    tokens = 2 * ht
    rank, width = b.shape
    lines, across = pack.shape[0] - rank, pack.shape[1]
    fac[...] = halves(ao[...], at[...], half)
    xs[:ht, :] = xo[...]
    xs[ht:tokens, :] = xt[...]
    xs[tokens:, :] = fac[...]
    ys[:ht, :] = yo[...]
    ys[ht:, :] = yt[...]
    lx = two_parts(dot(xs[:tokens, :], fac[...], NT))
    gram = two_parts(dot(fac[...], fac[...], NT))
    pack[lines:, :] = dot(ys[...], fac[...], NT).T
    for j in range(0, width, nb):
        cut = slice(j, j + nb)
        wv, bv = w[:, cut], b[:, cut]
        both_b = jnp.concatenate([bv, bv], axis=0)
        total = dot(xs[...], wv)
        res[...] = total[:tokens] + dot(lx, both_b)
        wf = wv.astype(f32)
        squares = jnp.sum((wf * wf).reshape(wf.shape[0] // 8, 8, nb), axis=0)
        cross = 2.0 * total[tokens:] + dot(gram, both_b)
        cross = bv.astype(f32) * cross
        for r in range(0, rank, 8):
            squares = squares + cross[r : r + 8]
        squares = jnp.sum(squares, axis=0, keepdims=True)
        for i in range(0, nb, across):
            at_line = (j + i) // across
            pack[at_line : at_line + 1, :] = squares[:, i : i + across]
        for k in range(count):
            at_row = place_of(jnp.bitwise_xor(me, k), half, count) * rows
            piece = res[pl.ds(pl.multiple_of(at_row, rows), rows), :]
            outs[k][:, cut] = piece.astype(outs[k].dtype)


def forward(count, rows, xo, xt, yo, yt, ao, at, b, w):
    ff, width = w.shape
    tokens = 2 * xo.shape[0]
    rank = b.shape[0]
    nb = block_of(width, 512)
    return whole_call(
        functools.partial(forward_kernel, count, rows, nb),
        (xo, xt, yo, yt, ao, at, b, w),
        [shaped((rows, width), f32 if k == 0 else bf16) for k in range(count)]
        + [
            shaped((width // tokens + rank, tokens), f32),
            shaped((tokens, ff), bf16),
            shaped((rank, ff), bf16),
        ],
        [pltpu.VMEM((tokens + rank, ff), bf16), pltpu.VMEM((tokens, nb), f32)],
        2 * tokens * ff * width,
        2 * ff * width,
    )


def again_kernel(nb, ys, pack, b, w, out):
    rank, width = b.shape
    ly = two_parts(pack[pack.shape[0] - rank :, :].T)
    for j in range(0, width, nb):
        cut = slice(j, j + nb)
        both_b = jnp.concatenate([b[:, cut], b[:, cut]], axis=0)
        out[:, cut] = dot(ys[...], w[:, cut]) + dot(ly, both_b)


def again(ys, pack, b, w):
    ff, width = w.shape
    tokens = ys.shape[0]
    return whole_call(
        functools.partial(again_kernel, block_of(width, 512)),
        (ys, pack, b, w),
        [shaped((tokens, width), f32)],
        (),
        2 * tokens * ff * width,
        2 * ff * width,
    )[0]


def join_kernel(one, two, out):
    out[...] = one[...] + two[...]


def join(one, two):
    return whole_call(join_kernel, (one, two), [shaped(one.shape, f32)])[0]


def prepare_kernel(count, rows, *refs):
    cots = refs[:count]
    packs, mag, r, b = refs[count : count + 2], *refs[count + 2 : count + 5]
    sc, ad, adapt, low, magpack, norms = refs[count + 5 :]
    half = lax.axis_index("section") % 2
    me = lax.axis_index("tensor")
    rank = b.shape[0]
    _, width = sc.shape
    total = packs[0][...] + packs[1][...]
    lines = total.shape[0] - rank
    across = total.shape[1]
    sqr = jnp.sqrt(jnp.maximum(total[:lines], 0.0) + epsilon)
    for i in range(lines):
        norms[0:1, i * across : (i + 1) * across] = sqr[i : i + 1, :]
    scale = mag[...] / norms[0:1, :]
    norms[1:2, :] = scale
    mags = jnp.zeros((8, width), f32)
    for k in range(count):
        at_row = place_of(jnp.bitwise_xor(me, k), half, count) * rows
        spot = pl.ds(pl.multiple_of(at_row, rows), rows)
        cot = cots[k][...].astype(f32)
        sc[spot, :] = (cot * scale).astype(bf16)
        mags = mags + jnp.sum((cot * r[spot, :]).reshape(rows // 8, 8, width), axis=0)
    mags = jnp.sum(mags, axis=0, keepdims=True)
    for i in range(lines):
        magpack[i : i + 1, :] = mags[:, i * across : (i + 1) * across]
    part = dot(sc[...], b[...], NT)
    adapt[...] = part
    ad[...] = two_parts(part)
    low[...] = total[lines:].astype(bf16)


def prepare(count, rows, cots, packs, mag, r, b):
    width = b.shape[1]
    tokens = rows * count
    rank = b.shape[0]
    return whole_call(
        functools.partial(prepare_kernel, count, rows),
        (*cots, *packs, mag, r, b),
        [
            shaped((tokens, width), bf16),
            shaped((tokens, 2 * rank), bf16),
            shaped((tokens, rank), f32),
            shaped((rank, tokens), bf16),
            shaped((width // tokens, tokens), f32),
            shaped((2, width), f32),
        ],
        moved=8 * tokens * width,
    )


def backward_kernel(rb, sc, ad, fac, w, own, send):
    half_tokens = own.shape[0]
    for j in range(0, w.shape[0], rb):
        cut = slice(j, j + rb)
        both_a = jnp.concatenate([fac[:, cut], fac[:, cut]], axis=0)
        out = dot(sc[...], w[cut, :], NT) + dot(ad[...], both_a)
        own[:, cut] = out[:half_tokens]
        send[:, cut] = out[half_tokens:].astype(bf16)


def backward(sc, ad, fac, w):
    ff, width = w.shape
    tokens = sc.shape[0]
    return whole_call(
        functools.partial(backward_kernel, block_of(ff, 512)),
        (sc, ad, fac, w),
        [shaped((tokens // 2, ff), f32), shaped((tokens // 2, ff), bf16)],
        (),
        2 * tokens * ff * width,
        2 * ff * width,
    )


def adapters_kernel(adapt, got_adapt, ys, low, sc, ga, gb):
    half = lax.axis_index("section") % 2
    tokens, rank = adapt.shape
    ht, hr = tokens // 2, rank // 2
    first = adapt[:ht, :] + got_adapt[ht:, :]
    second = adapt[ht:, :] + got_adapt[:ht, :]
    cot = jnp.concatenate([first, second], axis=0)
    cot = jnp.where(half == 0, cot[:, :hr], cot[:, hr:]).astype(bf16)
    ga[...] = dot(cot, ys[...], TN)
    gb[...] = dot(low[...], sc[...])


def adapters(adapt, got_adapt, ys, low, sc):
    rank = adapt.shape[1]
    return whole_call(
        adapters_kernel,
        (adapt, got_adapt, ys, low, sc),
        [shaped((rank // 2, ys.shape[1]), f32), shaped((rank, sc.shape[1]), f32)],
        moved=2 * ys.size,
    )


def emit_kernel(count, *refs):
    parts = refs[:count]
    carried, embedded, norms, out = refs[count:]
    slot = lax.axis_index("section")
    half = slot % 2
    width = out.shape[1]
    here = embedded[:, pl.ds(pl.multiple_of(half * width, width), width)].astype(f32)
    inflow = jnp.where(slot < 2, here, carried[...].astype(f32))
    total = parts[0][...]
    for k in range(1, count):
        total = total + parts[k][...].astype(f32)
    out[...] = (inflow + total * norms[1:2, :]).astype(bf16)


def emit(count, parts, carried, embedded, norms):
    return whole_call(
        functools.partial(emit_kernel, count),
        (*parts, carried, embedded, norms),
        [shaped(carried.shape, bf16)],
        moved=8 * carried.size * 2,
    )[0]


def finish_kernel(count, *refs):
    own, got = refs[:2]
    mags = refs[2 : 2 + count]
    norms = refs[2 + count]
    hidden, gm = refs[3 + count :]
    hidden[...] = (own[...] + got[...].astype(f32)).astype(bf16)
    total = mags[0][...]
    for k in range(1, count):
        total = total + mags[k][...]
    across = total.shape[1]
    for i in range(total.shape[0]):
        cut = slice(i * across, (i + 1) * across)
        gm[:, cut] = total[i : i + 1, :] / norms[0:1, cut]


def finish(count, own, got, mags, norms):
    return whole_call(
        functools.partial(finish_kernel, count),
        (own, got, *mags, norms),
        [shaped(own.shape, bf16), shaped((1, norms.shape[1]), f32)],
        moved=12 * own.size,
    )


def local(
    frozen,
    adapter_a,
    adapter_b,
    magnitude,
    hidden_fwd,
    carried,
    embedded,
    hidden_bwd,
    returned,
    head_grad,
):
    w, ao, b, xo, yo = frozen[0], adapter_a[0], adapter_b[0], hidden_fwd[0], hidden_bwd[0]
    slots = lax.axis_size("section")
    count = lax.axis_size("tensor")
    rows = carried.shape[1]

    def swap(array):
        return lax.ppermute(array, "section", [(i, i ^ 1) for i in range(slots)])

    def across(array, k):
        return lax.ppermute(array, "tensor", [(i, i ^ k) for i in range(count)])

    def shift(array, k):
        pairs = [
            (((s + 2) % slots) * count + t, s * count + (t ^ k))
            for s in range(slots)
            for t in range(count)
        ]
        return lax.ppermute(array, ("section", "tensor"), pairs)

    leaving = choose(returned[0], head_grad, 4 * rows * count * w.size)
    xt, at, yt = swap(xo), swap(ao), swap(yo)
    cots = [None] * count
    for k in range(count):
        direct = k < 2 or k % 2 == 0
        cots[k] = shift(leaving, k) if direct else across(cots[k - 1], 1)
    arriving = lax.ppermute(carried[0], "section", [(i, (i + 2) % slots) for i in range(slots)])
    *parts, pack, ys, fac = forward(count, rows, xo, xt, yo, yt, ao, at, b, w)
    for k in range(1, count):
        parts[k] = across(parts[k], k)
    got = across(pack, 1)
    r = again(ys, pack, b, w)
    for k in (2**n for n in range(1, count.bit_length() - 1)):
        pack = join(pack, got)
        got = across(pack, k)
    sc, ad, adapt, low, magpack, norms = prepare(
        count, rows, cots, (pack, got), magnitude, r, b
    )
    got_adapt = swap(adapt)
    mags = [magpack]
    for k in range(1, count):
        mags.append(across(magpack, k))
    own, send = backward(sc, ad, fac, w)
    got = swap(send)
    ga, gb = adapters(adapt, got_adapt, ys, low, sc)
    out = emit(count, parts, arriving, embedded, norms)
    hidden, gm = finish(count, own, got, mags, norms)
    return (out[None], gm, ga[None], gb[None], hidden[None])


def solution(mesh):
    placed = (
        P("section", "tensor", None),
        P("section", None, "tensor"),
        P("section", None, None),
        P("section", None),
        P("section", None, "tensor"),
        P("section", "tensor", None),
        P("tensor", None),
        P("section", None, "tensor"),
        P("section", "tensor", None),
        P("tensor", None),
    )

    return jax.shard_map(
        local,
        mesh=mesh,
        in_specs=placed,
        out_specs=(
            P("section", "tensor", None),
            P("section", None),
            P("section", None, "tensor"),
            P("section", None, None),
            P("section", None, "tensor"),
        ),
        check_vma=False,
    )
```
